768 devices in a mesh: dp: 24 (over z, core), vocab: 32 (over y, x).
Axes of the slice: x: 4, y: 8, z: 12, core: 2. Of those that a mesh axis runs over, the one named last changes fastest.
Arguments:
- tokens_in: bfloat16 [3072, 8192], P('dp'), may hold values from -80 to 80
- gain: float32 [8192], replicated, may hold values from 0.5 to 1.5
- head_weight: bfloat16 [8192, 16896], P(None, 'vocab'), may hold values from -0.5 to 0.5
- teacher_ids: int32 [3072, 16], P('dp'), may hold values from 0 to 16895
- teacher_weight: float32 [3072, 16], P('dp'), may hold values from 0.05 to 1
- labels: int32 [3072], P('dp'), may hold values from 0 to 16895
Outputs:
- token_loss: float32 [3072], P('dp')
- grad_input: bfloat16 [3072, 8192], P('dp', 'vocab')
- head_grad: float32 [528, 32, 8192], P('dp', 'vocab')
The draws below stay inside these ranges and needn't reach their ends.
All inputs are finite; a program needn't handle non-finite values.
Results may differ from the reference program's by a relative error of at most 0.015.
Values may be sent and summed in bfloat16 or wider, within the bound.
No kernel may reach another device: no remote copies, remote signals or barrier semaphores. Data moves between devices by JAX's collectives and lax.ppermute only.
A program may use at most 64 MiB of HBM per device.

```python
import math
import jax
import jax.numpy as jnp
import numpy as np
from jax import lax

D = 8192
V = 16896
TOPK = 16
TOK_DEV = 128
TOKENS = 3072
N_DP = 24
N_VOCAB = 32


def pair_vectors(key):
    strength = jnp.array([120.0, 160.0, 200.0, 250.0], jnp.float32)
    noise = jnp.clip(jax.random.normal(jax.random.fold_in(key, 7), (4, D), jnp.float32), -3.0, 3.0)
    return (noise, strength)


def draw_head_weight(key, part):
    base = jax.random.normal(jax.random.fold_in(key, 1), (D, V), jnp.float32) * (3.0 / math.sqrt(D))
    base = jnp.clip(base, -0.25, 0.25)
    noise, strength = pair_vectors(key)
    aligned = noise * (strength[:, None] / D)
    shrink = 1.0 - 2.0 / strength
    columns = jnp.arange(4, dtype=jnp.int32) * (V // 4) + 5
    base = base.at[:, columns].set(jnp.transpose(aligned))
    base = base.at[:, columns + 1].set(jnp.transpose(aligned * shrink[:, None]))
    return base.astype(jnp.bfloat16)


def draw_tokens_in(key, part):
    noise = jax.random.normal(jax.random.fold_in(key, 2), (TOKENS, D), jnp.float32)
    row_scales = jnp.exp(jax.random.uniform(jax.random.fold_in(key, 3), (TOKENS,), jnp.float32, 0.0, math.log(10.0)))
    col_scales = jnp.exp(jax.random.uniform(jax.random.fold_in(key, 5), (D,), jnp.float32, 0.0, math.log(10.0)))
    values = noise * row_scales[:, None] * col_scales[None, :]
    pair_noise, strength = pair_vectors(key)
    chosen = jnp.arange(4, dtype=jnp.int32) * (TOKENS // 4) + 3
    values = values.at[chosen].set(pair_noise * 10.0)
    return jnp.clip(values, -80.0, 80.0).astype(jnp.bfloat16)


def touch_ends(values, own_key, least, high):
    index_at = [jax.random.randint(jax.random.fold_in(own_key, axis), (), 0, length) for axis, length in enumerate(values.shape)]
    main_axis = values.shape.index(max(values.shape))
    next_to = index_at[:main_axis] + [(index_at[main_axis] + 1) % values.shape[main_axis]] + index_at[main_axis + 1:]
    return values.at[tuple(index_at)].set(least).at[tuple(next_to)].set(high)


def level_of(rng, shape, split, least, largest):
    loudness, own = 1.0, jax.random.fold_in(rng, 6)
    for dim, parts in split:
        heights = jnp.exp(jax.random.uniform(jax.random.fold_in(own, dim), (parts,), jnp.float32, least / len(split), largest / len(split)))
        loudness = loudness * jnp.repeat(heights, shape[dim] // parts).reshape([-1 if axis == dim else 1 for axis in range(len(shape))])
    return loudness


def cumulative_ranks(amount, skew):
    loads = [(1 << 20) // math.isqrt(rank ** skew) + 1 for rank in range(1, amount + 1)]
    scale = 1 + sum(loads) // (1 << 30)
    return np.cumsum(np.array([max(1, weight // scale) for weight in loads]))


def ranked_ids(key, extent, amount, lean):
    listing = cumulative_ranks(amount, lean)
    lot = jax.random.randint(jax.random.fold_in(key, 1), extent, 0, int(listing[amount - 1]))
    grade = jnp.searchsorted(jnp.asarray(listing, jnp.int32), lot, side="right")
    return jax.random.permutation(jax.random.fold_in(key, 2), amount)[grade].astype(jnp.int32)


def setup_inputs(seed: int = 0) -> dict:
    key_list = jax.random.split(jax.random.key(seed), 7)
    tokens_in = draw_tokens_in(jax.random.fold_in(key_list[6], 71), 0)
    gain = jnp.clip(1.0 + 0.1 * jax.random.normal(key_list[1], (D,), jnp.float32), 0.5, 1.5)
    head_weight = draw_head_weight(jax.random.fold_in(key_list[6], 71), 0)
    teacher_ids = touch_ends(ranked_ids(key_list[3], (TOKENS, TOPK), V, 2), jax.random.fold_in(key_list[3], 3), 0, V - 1).astype(jnp.int32)
    teacher_weight = jnp.clip(jnp.exp(math.log(1.0) - 2.9957323 * jax.random.uniform(key_list[4], (TOKENS, TOPK), jnp.float32) ** level_of(key_list[4], (TOKENS, TOPK), ((0, 24),), -0.2, 0.2)), 0.05, 1.0)
    labels = touch_ends(ranked_ids(key_list[5], (TOKENS,), V, 2), jax.random.fold_in(key_list[5], 3), 0, V - 1).astype(jnp.int32)
    return dict(tokens_in=tokens_in, gain=gain, head_weight=head_weight, teacher_ids=teacher_ids, teacher_weight=teacher_weight, labels=labels)


LABEL_SHARE = 0.5
EPS = 1e-05

def normalize(tokens_in, gain):
    as_float = tokens_in.astype(jnp.float32)
    row_scale = jnp.sqrt(lax.optimization_barrier(jnp.mean(as_float * as_float, axis=1, keepdims=True)) + EPS)
    normed = (as_float / row_scale * gain[None, :]).astype(jnp.bfloat16)
    return (as_float, row_scale, normed)

def targets(teacher_ids, teacher_probs, labels, col_start, col_width):
    columns = col_start + jnp.arange(col_width, dtype=jnp.int32)
    matches = (teacher_ids[:, :, None] == columns[None, None, :]).astype(jnp.float32)
    teacher_part = lax.optimization_barrier(jnp.sum(teacher_probs[:, :, None] * matches, axis=1))
    label_part = (labels[:, None] == columns[None, :]).astype(jnp.float32)
    return (1.0 - LABEL_SHARE) * teacher_part + LABEL_SHARE * label_part

def round_half(values):
    return lax.optimization_barrier(values.astype(jnp.bfloat16)).astype(jnp.float32)

def reference(tokens_in, gain, head_weight, teacher_ids, teacher_weight, labels):
    as_float, row_scale, normed = normalize(tokens_in, gain)
    logits = jnp.dot(normed, head_weight, preferred_element_type=jnp.float32)
    teacher_probs = teacher_weight / lax.optimization_barrier(jnp.sum(teacher_weight, axis=1, keepdims=True))
    col_width = V // N_VOCAB

    def one_block(block_index):
        return targets(teacher_ids, teacher_probs, labels, (block_index * col_width).astype(jnp.int32), col_width)
    blocks = lax.map(one_block, jnp.arange(N_VOCAB, dtype=jnp.int32))
    target = jnp.transpose(blocks, (1, 0, 2)).reshape(TOKENS, V)
    row_top = lax.optimization_barrier(jnp.max(logits, axis=1))
    total_exp = lax.optimization_barrier(jnp.sum(jnp.exp(logits - row_top[:, None]), axis=1))
    total_dot = lax.optimization_barrier(jnp.sum(target * logits, axis=1))
    lse = row_top + jnp.log(total_exp)
    token_loss = (1.0 - LABEL_SHARE) * lax.optimization_barrier(jnp.sum(teacher_probs * jnp.log(teacher_probs), axis=1)) - total_dot + lse
    dlogits = (jnp.exp(logits - lse[:, None]) - target).astype(jnp.bfloat16)

    def add_block(block_index, running):
        first = (block_index * col_width).astype(jnp.int32)
        grad_block = lax.dynamic_slice_in_dim(dlogits, first, col_width, 1)
        weight_block = lax.dynamic_slice_in_dim(head_weight, first, col_width, 1)
        partial_value = lax.dot_general(grad_block, weight_block, (((1,), (1,)), ((), ())), preferred_element_type=jnp.float32)
        return running + round_half(partial_value)
    dhidden = lax.fori_loop(0, N_VOCAB, add_block, jnp.zeros((TOKENS, D), jnp.float32))
    scaled = dhidden * gain[None, :]
    inner_sum = lax.optimization_barrier(jnp.sum(scaled * as_float, axis=1, keepdims=True))
    grad_input = (scaled / row_scale - as_float * inner_sum / (D * row_scale * row_scale * row_scale)).astype(jnp.bfloat16)

    def add_replica(replica, running):
        first = (replica * TOK_DEV).astype(jnp.int32)
        grad_block = lax.dynamic_slice_in_dim(dlogits, first, TOK_DEV, 0)
        normed_block = lax.dynamic_slice_in_dim(normed, first, TOK_DEV, 0)
        partial_value = lax.dot_general(grad_block, normed_block, (((0,), (0,)), ((), ())), preferred_element_type=jnp.float32)
        return running + round_half(partial_value)
    head_total = lax.fori_loop(0, N_DP, add_replica, jnp.zeros((V, D), jnp.float32))
    head_grad = jnp.transpose(head_total.reshape(N_VOCAB, col_width, D), (1, 0, 2))
    return (token_loss, grad_input, head_grad)
```

```python
import jax
import jax.numpy as jnp
from jax import lax
from jax.sharding import Mesh, PartitionSpec as P

LABEL_SHARE = 0.5
EPS = 1e-05
NZ, NC, NY, NX = 12, 2, 8, 4


def normalize(tokens_in, gain):
    as_float = tokens_in.astype(jnp.float32)
    row_scale = jnp.sqrt(jnp.mean(as_float * as_float, axis=1, keepdims=True) + EPS)
    normed = (as_float / row_scale * gain[None, :]).astype(jnp.bfloat16)
    return (row_scale, normed)


def targets(teacher_ids, teacher_probs, labels, col_start, col_width):
    columns = col_start + jnp.arange(col_width, dtype=jnp.int32)
    matches = (teacher_ids[:, :, None] == columns[None, None, :]).astype(jnp.float32)
    teacher_part = jnp.sum(teacher_probs[:, :, None] * matches, axis=1)
    label_part = (labels[:, None] == columns[None, :]).astype(jnp.float32)
    return (1.0 - LABEL_SHARE) * teacher_part + LABEL_SHARE * label_part


def local(tokens_in, gain, head_weight, teacher_ids, teacher_weight, labels):
    tokens, features = tokens_in.shape
    col_width = head_weight.shape[1]
    n_vocab = NY * NX
    block = lax.axis_index("y") * NX + lax.axis_index("x")
    core = lax.axis_index("c")
    swap = [(0, 1), (1, 0)]
    row_scale, normed = normalize(tokens_in, gain)
    other_normed = lax.ppermute(normed, "c", swap)
    logits = jnp.dot(normed, head_weight, preferred_element_type=jnp.float32)
    teacher_probs = teacher_weight / jnp.sum(teacher_weight, axis=1, keepdims=True)
    target = targets(teacher_ids, teacher_probs, labels, block * col_width, col_width)
    top = jnp.max(logits, axis=1)
    exps = jnp.exp(logits - top[:, None])
    stats = jnp.stack(
        [top, jnp.sum(exps, axis=1), jnp.sum(target * logits, axis=1), jnp.sum(exps * logits, axis=1)]
    )
    with jax.named_scope("stats"):
        stats = lax.all_to_all(
            jnp.broadcast_to(stats[None], (n_vocab,) + stats.shape), ("y", "x"), 0, 0
        )
    row_top = jnp.max(stats[:, 0], axis=0)
    weight = jnp.exp(stats[:, 0] - row_top[None])
    total_exp = jnp.sum(weight * stats[:, 1], axis=0)
    total_dot = jnp.sum(stats[:, 2], axis=0)
    mean_logit = jnp.sum(weight * stats[:, 3], axis=0) / total_exp
    lse = row_top + jnp.log(total_exp)
    token_loss = (
        (1.0 - LABEL_SHARE) * jnp.sum(teacher_probs * jnp.log(teacher_probs), axis=1)
        - total_dot
        + lse
    )
    dlogits = (jnp.exp(logits - lse[:, None]) - target).astype(jnp.bfloat16)

    rows = col_width // (NZ * NC)
    by_owner = dlogits.reshape(tokens, NZ, NC, rows)
    mine = lax.dynamic_index_in_dim(by_owner, core, 2, False).reshape(tokens, NZ * rows)
    theirs = lax.dynamic_index_in_dim(by_owner, 1 - core, 2, False).reshape(tokens, NZ * rows)
    other_mine = lax.ppermute(theirs, "c", swap)

    partial_value = lax.dot_general(
        dlogits, head_weight, (((1,), (1,)), ((), ())), preferred_element_type=jnp.float32
    ).astype(jnp.bfloat16)
    width = features // n_vocab
    pieces = partial_value.reshape(tokens, n_vocab, width).transpose(1, 0, 2)
    with jax.named_scope("dhid"):
        pieces = lax.all_to_all(pieces, ("y", "x"), 0, 0)

    head_term = lax.dot_general(
        jnp.concatenate([mine, other_mine], axis=0),
        jnp.concatenate([normed, other_normed], axis=0),
        (((0,), (0,)), ((), ())),
        preferred_element_type=jnp.float32,
    )
    with jax.named_scope("ring"):
        summed = lax.psum_scatter(
            head_term.astype(jnp.bfloat16), "z", scatter_dimension=0, tiled=True
        )
    head_grad = summed.astype(jnp.float32)[:, None, :]

    dhidden = jnp.sum(pieces.astype(jnp.float32), axis=0)
    local_tokens = lax.dynamic_slice_in_dim(tokens_in, block * width, width, 1).astype(jnp.float32)
    local_gain = lax.dynamic_slice_in_dim(gain, block * width, width, 0)
    inner_sum = row_scale * (mean_logit - total_dot)[:, None]
    cubed = row_scale * row_scale * row_scale
    grad_input = (
        dhidden * local_gain[None, :] / row_scale - local_tokens * inner_sum / (features * cubed)
    ).astype(jnp.bfloat16)
    return (token_loss, grad_input, head_grad)


def solution(mesh):
    fine = Mesh(mesh.devices.reshape(NZ, NC, NY, NX), ("z", "c", "y", "x"))
    dp, vocab = ("z", "c"), ("y", "x")
    in_specs = (P(dp, None), P(), P(None, vocab), P(dp, None), P(dp, None), P(dp))
    out_specs = (P(dp), P(dp, vocab), P(dp, vocab, None))
    return jax.shard_map(local, mesh=fine, in_specs=in_specs, out_specs=out_specs, check_vma=False)
```

```python
import jax
import jax.numpy as jnp
from jax import lax
from jax.sharding import Mesh, PartitionSpec as P


LABEL_SHARE = 0.5
EPS = 1e-05
NZ, NC, NY, NX = 12, 2, 8, 4


def normalize(tokens_in, gain):
    as_float = tokens_in.astype(jnp.float32)
    row_scale = jnp.sqrt(jnp.mean(as_float * as_float, axis=1, keepdims=True) + EPS)
    normed = (as_float / row_scale * gain[None, :]).astype(jnp.bfloat16)
    return (row_scale, normed)


def targets(teacher_ids, teacher_probs, labels, col_start, col_width):
    columns = col_start + jnp.arange(col_width, dtype=jnp.int32)
    matches = (teacher_ids[:, :, None] == columns[None, None, :]).astype(jnp.float32)
    teacher_part = jnp.sum(teacher_probs[:, :, None] * matches, axis=1)
    label_part = (labels[:, None] == columns[None, :]).astype(jnp.float32)
    return (1.0 - LABEL_SHARE) * teacher_part + LABEL_SHARE * label_part


def local(tokens_in, gain, head_weight, teacher_ids, teacher_weight, labels):
    tokens, features = tokens_in.shape
    col_width = head_weight.shape[1]
    n_vocab = NY * NX
    block = lax.axis_index("y") * NX + lax.axis_index("x")
    core = lax.axis_index("c")
    swap = [(0, 1), (1, 0)]
    row_scale, normed = normalize(tokens_in, gain)
    other_normed = lax.ppermute(normed, "c", swap)
    logits = jnp.dot(normed, head_weight, preferred_element_type=jnp.float32)
    teacher_probs = teacher_weight / jnp.sum(teacher_weight, axis=1, keepdims=True)
    target = targets(teacher_ids, teacher_probs, labels, block * col_width, col_width)
    top = jnp.max(logits, axis=1)
    exps = jnp.exp(logits - top[:, None])
    stats = jnp.stack(
        [top, jnp.sum(exps, axis=1), jnp.sum(target * logits, axis=1), jnp.sum(exps * logits, axis=1)]
    )
    stats = lax.all_to_all(
        jnp.broadcast_to(stats[None], (n_vocab,) + stats.shape), ("y", "x"), 0, 0
    )
    row_top = jnp.max(stats[:, 0], axis=0)
    weight = jnp.exp(stats[:, 0] - row_top[None])
    total_exp = jnp.sum(weight * stats[:, 1], axis=0)
    total_dot = jnp.sum(stats[:, 2], axis=0)
    mean_logit = jnp.sum(weight * stats[:, 3], axis=0) / total_exp
    lse = row_top + jnp.log(total_exp)
    token_loss = (
        (1.0 - LABEL_SHARE) * jnp.sum(teacher_probs * jnp.log(teacher_probs), axis=1)
        - total_dot
        + lse
    )
    dlogits = (jnp.exp(logits - lse[:, None]) - target).astype(jnp.bfloat16)

    rows = col_width // (NZ * NC)
    by_owner = jnp.pad(dlogits.reshape(tokens, NZ, NC, rows), ((0, 0), (0, 0), (0, 0), (0, 2)))
    mine = lax.dynamic_index_in_dim(by_owner, core, 2, False).reshape(tokens, -1)
    theirs = lax.dynamic_index_in_dim(by_owner, 1 - core, 2, False).reshape(tokens, -1)
    other_mine = lax.ppermute(theirs, "c", swap)

    partial_value = lax.dot_general(
        dlogits, head_weight, (((1,), (1,)), ((), ())), preferred_element_type=jnp.float32
    ).astype(jnp.bfloat16)
    width = features // n_vocab
    pieces = partial_value.reshape(tokens, n_vocab, width).transpose(1, 0, 2)
    pieces = lax.all_to_all(pieces, ("y", "x"), 0, 0)

    head_term = lax.dot_general(
        jnp.concatenate([mine, other_mine], axis=0),
        jnp.concatenate([normed, other_normed], axis=0),
        (((0,), (0,)), ((), ())),
        preferred_element_type=jnp.float32,
    )
    summed = lax.psum_scatter(head_term.astype(jnp.bfloat16), "z", scatter_dimension=0, tiled=True)
    head_grad = summed[:rows].astype(jnp.float32)[:, None, :]

    dhidden = jnp.sum(pieces.astype(jnp.float32), axis=0)
    local_tokens = lax.dynamic_slice_in_dim(tokens_in, block * width, width, 1).astype(jnp.float32)
    local_gain = lax.dynamic_slice_in_dim(gain, block * width, width, 0)
    inner_sum = row_scale * (mean_logit - total_dot)[:, None]
    cubed = row_scale * row_scale * row_scale
    grad_input = (
        dhidden * local_gain[None, :] / row_scale - local_tokens * inner_sum / (features * cubed)
    ).astype(jnp.bfloat16)
    return (token_loss, grad_input, head_grad)


def solution(mesh):
    fine = Mesh(mesh.devices.reshape(NZ, NC, NY, NX), ("z", "c", "y", "x"))
    dp, vocab = ("z", "c"), ("y", "x")
    in_specs = (P(dp, None), P(), P(None, vocab), P(dp, None), P(dp, None), P(dp))
    out_specs = (P(dp), P(dp, vocab), P(dp, vocab, None))
    return jax.shard_map(local, mesh=fine, in_specs=in_specs, out_specs=out_specs, check_vma=False)
```

```python
import jax
import jax.numpy as jnp
from jax import lax
from jax.experimental import pallas as pl
from jax.experimental.pallas import tpu as pltpu
from jax.sharding import Mesh, PartitionSpec as P


LABEL_SHARE = 0.5
EPS = 1e-05
NZ, NC, NY, NX = 12, 2, 8, 4


def front_kernel(
    start_ref, x_hbm, gain_ref, w_hbm, ids_ref, weight_ref, label_ref,
    normed_hbm, scale_ref, logits_ref, target_ref, stats_ref,
    x_buf, w_buf, normed_buf, x_sem, w_sem, out_sem,
):
    tokens, features = x_buf.shape
    cols = w_buf.shape[0]
    parts = w_sem.shape[0]
    rows = cols // parts
    step = 1024
    copy_x = pltpu.make_async_copy(x_hbm, x_buf, x_sem)
    copy_x.start()
    copies = []
    for p in range(parts):
        part = pl.ds(p * rows, rows)
        copies.append(pltpu.make_async_copy(w_hbm.at[part], w_buf.at[part], w_sem.at[p]))
        copies[-1].start()

    probs = weight_ref[...] / jnp.sum(weight_ref[...], axis=0, keepdims=True)
    columns = start_ref[0] + lax.broadcasted_iota(jnp.int32, (cols, tokens), 0)
    teacher_part = jnp.zeros((cols, tokens), jnp.float32)
    for k in range(ids_ref.shape[0]):
        teacher_part += jnp.where(ids_ref[k : k + 1, :] == columns, probs[k : k + 1, :], 0.0)
    label_part = jnp.where(label_ref[...] == columns, LABEL_SHARE, 0.0)
    target_ref[...] = (1.0 - LABEL_SHARE) * teacher_part + label_part

    copy_x.wait()
    total = jnp.zeros((tokens, 128), jnp.float32)
    for f in range(0, features, step):
        chunk = x_buf[:, f : f + step].astype(jnp.float32)
        chunk = chunk * chunk
        for g in range(0, step, 128):
            total += chunk[:, g : g + 128]
    scale = jnp.sqrt(jnp.sum(total, axis=1, keepdims=True) / features + EPS)
    scale_ref[...] = scale
    inverse = 1.0 / scale
    for f in range(0, features, step):
        chunk = x_buf[:, f : f + step].astype(jnp.float32)
        normed_buf[:, f : f + step] = (chunk * inverse * gain_ref[:, f : f + step]).astype(
            jnp.bfloat16
        )
    copy_out = pltpu.make_async_copy(normed_buf, normed_hbm, out_sem)
    copy_out.start()
    for p in range(parts):
        copies[p].wait()
        part = pl.ds(p * rows, rows)
        logits_ref[part, :] = lax.dot_general(
            w_buf[part, :],
            normed_buf[...],
            (((1,), (1,)), ((), ())),
            preferred_element_type=jnp.float32,
        )
    logits = logits_ref[...]
    top = jnp.max(logits, axis=0, keepdims=True)
    exps = jnp.exp(logits - top)
    stats_ref[0:1, :] = top
    stats_ref[1:2, :] = jnp.sum(exps, axis=0, keepdims=True)
    stats_ref[2:3, :] = jnp.sum(target_ref[...] * logits, axis=0, keepdims=True)
    stats_ref[3:4, :] = jnp.sum(exps * logits, axis=0, keepdims=True)
    copy_out.wait()


def front(tokens_in, gain, weight_t, ids_t, teacher_t, labels, start):
    tokens, features = tokens_in.shape
    cols = weight_t.shape[0]
    parts = 3
    vmem = pl.BlockSpec(memory_space=pltpu.VMEM)
    hbm = pl.BlockSpec(memory_space=pltpu.HBM)
    return pl.pallas_call(
        front_kernel,
        name="front",
        out_shape=(
            jax.ShapeDtypeStruct((tokens, features), jnp.bfloat16),
            jax.ShapeDtypeStruct((tokens, 1), jnp.float32),
            jax.ShapeDtypeStruct((cols, tokens), jnp.float32),
            jax.ShapeDtypeStruct((cols, tokens), jnp.float32),
            jax.ShapeDtypeStruct((4, tokens), jnp.float32),
        ),
        in_specs=[pl.BlockSpec(memory_space=pltpu.SMEM), hbm, vmem, hbm, vmem, vmem, vmem],
        out_specs=(hbm, vmem, vmem, vmem, vmem),
        scratch_shapes=[
            pltpu.VMEM((tokens, features), jnp.bfloat16),
            pltpu.VMEM((cols, features), jnp.bfloat16),
            pltpu.VMEM((tokens, features), jnp.bfloat16),
            pltpu.SemaphoreType.DMA,
            pltpu.SemaphoreType.DMA((parts,)),
            pltpu.SemaphoreType.DMA,
        ],
        cost_estimate=pl.CostEstimate(
            flops=2 * tokens * features * cols,
            bytes_accessed=2 * features * (2 * tokens + cols),
            transcendentals=cols * tokens,
        ),
    )(start, tokens_in, gain, weight_t, ids_t, teacher_t, labels)


def back_kernel(dlogits_ref, w_ref, out_ref):
    width = out_ref.shape[2]
    for q in range(out_ref.shape[0]):
        out_ref[q] = jnp.dot(
            dlogits_ref[...],
            w_ref[:, q * width : (q + 1) * width],
            preferred_element_type=jnp.float32,
        ).astype(jnp.bfloat16)


def back(dlogits, weight_t, n_vocab):
    tokens, cols = dlogits.shape
    features = weight_t.shape[1]
    width = features // n_vocab
    group = 4
    return pl.pallas_call(
        back_kernel,
        name="back",
        grid=(n_vocab // group,),
        out_shape=jax.ShapeDtypeStruct((n_vocab, tokens, width), jnp.bfloat16),
        in_specs=[
            pl.BlockSpec((tokens, cols), lambda i: (0, 0)),
            pl.BlockSpec((cols, group * width), lambda i: (0, i)),
        ],
        out_specs=pl.BlockSpec((group, tokens, width), lambda i: (i, 0, 0)),
        cost_estimate=pl.CostEstimate(
            flops=2 * tokens * features * cols,
            bytes_accessed=2 * features * (tokens + cols),
            transcendentals=0,
        ),
    )(dlogits, weight_t)


def local(tokens_in, gain, head_weight, teacher_ids, teacher_weight, labels):
    tokens, features = tokens_in.shape
    col_width = head_weight.shape[1]
    n_vocab = NY * NX
    block = lax.axis_index("y") * NX + lax.axis_index("x")
    core = lax.axis_index("c")
    swap = [(0, 1), (1, 0)]
    weight_t = head_weight.T
    start = (block * col_width).astype(jnp.int32).reshape(1)
    normed, row_scale, logits, target, stats = front(
        tokens_in, gain[None], weight_t, teacher_ids.T, teacher_weight.T, labels[None], start
    )
    other_normed = lax.ppermute(normed, "c", swap)
    teacher_probs = teacher_weight / jnp.sum(teacher_weight, axis=1, keepdims=True)
    stats = lax.all_to_all(
        jnp.broadcast_to(stats[None], (n_vocab,) + stats.shape), ("y", "x"), 0, 0
    )
    row_top = jnp.max(stats[:, 0], axis=0)
    weight = jnp.exp(stats[:, 0] - row_top[None])
    total_exp = jnp.sum(weight * stats[:, 1], axis=0)
    total_dot = jnp.sum(stats[:, 2], axis=0)
    mean_logit = jnp.sum(weight * stats[:, 3], axis=0) / total_exp
    lse = row_top + jnp.log(total_exp)
    token_loss = (
        (1.0 - LABEL_SHARE) * jnp.sum(teacher_probs * jnp.log(teacher_probs), axis=1)
        - total_dot
        + lse
    )
    dlogits = (jnp.exp(logits - lse[None]) - target).astype(jnp.bfloat16)

    rows = col_width // (NZ * NC)
    by_owner = jnp.pad(dlogits.reshape(NZ, NC, rows, tokens), ((0, 0), (0, 0), (0, 2), (0, 0)))
    mine = lax.dynamic_index_in_dim(by_owner, core, 1, False).reshape(-1, tokens)
    theirs = lax.dynamic_index_in_dim(by_owner, 1 - core, 1, False).reshape(-1, tokens)
    other_mine = lax.ppermute(theirs, "c", swap)

    width = features // n_vocab
    pieces = back(dlogits.T, weight_t, n_vocab)
    pieces = lax.all_to_all(pieces, ("y", "x"), 0, 0)

    head_term = lax.dot_general(
        jnp.concatenate([mine, other_mine], axis=1),
        jnp.concatenate([normed, other_normed], axis=0),
        (((1,), (0,)), ((), ())),
        preferred_element_type=jnp.float32,
    )
    summed = lax.psum_scatter(head_term.astype(jnp.bfloat16), "z", scatter_dimension=0, tiled=True)
    head_grad = summed[:rows].astype(jnp.float32)[:, None, :]

    dhidden = jnp.sum(pieces.astype(jnp.float32), axis=0)
    local_tokens = lax.dynamic_slice_in_dim(tokens_in, block * width, width, 1).astype(jnp.float32)
    local_gain = lax.dynamic_slice_in_dim(gain, block * width, width, 0)
    inner_sum = row_scale * (mean_logit - total_dot)[:, None]
    cubed = row_scale * row_scale * row_scale
    grad_input = (
        dhidden * local_gain[None, :] / row_scale - local_tokens * inner_sum / (features * cubed)
    ).astype(jnp.bfloat16)
    return (token_loss, grad_input, head_grad)


def solution(mesh):
    fine = Mesh(mesh.devices.reshape(NZ, NC, NY, NX), ("z", "c", "y", "x"))
    dp, vocab = ("z", "c"), ("y", "x")
    in_specs = (P(dp, None), P(), P(None, vocab), P(dp, None), P(dp, None), P(dp))
    out_specs = (P(dp), P(dp, vocab), P(dp, vocab, None))
    return jax.shard_map(local, mesh=fine, in_specs=in_specs, out_specs=out_specs, check_vma=False)
```

```python
import jax
import jax.numpy as jnp
from jax import lax
from jax.experimental import pallas as pl
from jax.experimental.pallas import tpu as pltpu
from jax.sharding import Mesh, PartitionSpec as P


LABEL_SHARE = 0.5
EPS = 1e-05
NZ, NC, NY, NX = 12, 2, 8, 4
SPLIT = 6144


def front_kernel(
    start_ref, x_hbm, gain_ref, w_hbm, ids_ref, weight_ref, label_ref,
    low_hbm, high_hbm, scale_ref, logits_ref, target_ref, stats_ref,
    x_buf, w_ref, normed_buf, x_sem, w_sem, out_sem,
):
    tokens, features = x_buf.shape
    cols = w_ref.shape[0]
    parts = w_sem.shape[0]
    rows = cols // parts
    lines = 16
    copy_x = pltpu.make_async_copy(x_hbm, x_buf, x_sem)
    copy_x.start()

    def copy_w(p):
        part = pl.ds(p * rows, rows)
        return pltpu.make_async_copy(w_hbm.at[part], w_ref.at[part], w_sem.at[p])

    @pl.loop(0, parts)
    def _(p):
        copy_w(p).start()

    probs = weight_ref[...] / jnp.sum(weight_ref[...], axis=0, keepdims=True)

    @pl.loop(0, cols // lines)
    def _(r):
        part = pl.ds(pl.multiple_of(r * lines, lines), lines)
        columns = start_ref[0] + r * lines + lax.broadcasted_iota(jnp.int32, (lines, tokens), 0)
        teacher_part = jnp.zeros((lines, tokens), jnp.float32)
        for k in range(ids_ref.shape[0]):
            teacher_part += jnp.where(ids_ref[k : k + 1, :] == columns, probs[k : k + 1, :], 0.0)
        label_part = jnp.where(label_ref[...] == columns, LABEL_SHARE, 0.0)
        target_ref[part, :] = (1.0 - LABEL_SHARE) * teacher_part + label_part

    copy_x.wait()

    @pl.loop(0, tokens // lines)
    def _(r):
        part = pl.ds(pl.multiple_of(r * lines, lines), lines)
        totals = [jnp.zeros((lines, 128), jnp.float32) for _ in range(4)]
        for f in range(0, features, 128):
            chunk = x_buf[part, f : f + 128].astype(jnp.float32)
            totals[f // 128 % 4] += chunk * chunk
        total = (totals[0] + totals[1]) + (totals[2] + totals[3])
        scale = jnp.sqrt(jnp.sum(total, axis=1, keepdims=True) / features + EPS)
        scale_ref[part, :] = scale
        inverse = jnp.broadcast_to(1.0 / scale, (lines, 128))
        for f in range(0, features, 128):
            chunk = x_buf[part, f : f + 128].astype(jnp.float32)
            chunk = chunk * inverse * gain_ref[:, f : f + 128]
            normed_buf[part, f : f + 128] = chunk.astype(jnp.bfloat16)

    copy_low = pltpu.make_async_copy(normed_buf.at[:, :SPLIT], low_hbm, out_sem.at[0])
    copy_high = pltpu.make_async_copy(normed_buf.at[:, SPLIT:], high_hbm, out_sem.at[1])
    copy_low.start()
    copy_high.start()
    for p in range(parts):
        copy_w(p).wait()
        part = pl.ds(p * rows, rows)
        logits_ref[part, :] = lax.dot_general(
            w_ref[part, :],
            normed_buf[...],
            (((1,), (1,)), ((), ())),
            preferred_element_type=jnp.float32,
        )
    logits = logits_ref[...]
    top = jnp.max(logits, axis=0, keepdims=True)
    exps = jnp.exp(logits - top)
    local_stats = (
        top,
        jnp.sum(exps, axis=0, keepdims=True),
        jnp.sum(target_ref[...] * logits, axis=0, keepdims=True),
        jnp.sum(exps * logits, axis=0, keepdims=True),
    )
    for q, row in enumerate(local_stats):
        stats_ref[:, q, :] = jnp.broadcast_to(row, (stats_ref.shape[0], tokens))
    copy_low.wait()
    copy_high.wait()


def front(tokens_in, gain, weight_t, ids_t, teacher_t, labels, start, n_vocab):
    tokens, features = tokens_in.shape
    cols = weight_t.shape[0]
    parts = 3
    vmem = pl.BlockSpec(memory_space=pltpu.VMEM)
    hbm = pl.BlockSpec(memory_space=pltpu.HBM)
    return pl.pallas_call(
        front_kernel,
        name="front",
        out_shape=(
            jax.ShapeDtypeStruct((tokens, SPLIT), jnp.bfloat16),
            jax.ShapeDtypeStruct((tokens, features - SPLIT), jnp.bfloat16),
            jax.ShapeDtypeStruct((tokens, 1), jnp.float32),
            jax.ShapeDtypeStruct((cols, tokens), jnp.float32),
            jax.ShapeDtypeStruct((cols, tokens), jnp.float32),
            jax.ShapeDtypeStruct((n_vocab, 4, tokens), jnp.float32),
        ),
        in_specs=[pl.BlockSpec(memory_space=pltpu.SMEM), hbm, vmem, hbm, vmem, vmem, vmem],
        out_specs=(hbm, hbm, vmem, vmem, vmem, vmem),
        scratch_shapes=[
            pltpu.VMEM((tokens, features), jnp.bfloat16),
            pltpu.VMEM((cols, features), jnp.bfloat16),
            pltpu.VMEM((tokens, features), jnp.bfloat16),
            pltpu.SemaphoreType.DMA,
            pltpu.SemaphoreType.DMA((parts,)),
            pltpu.SemaphoreType.DMA((2,)),
        ],
        cost_estimate=pl.CostEstimate(
            flops=2 * tokens * features * cols,
            bytes_accessed=2 * features * (2 * tokens + cols),
            transcendentals=cols * tokens,
        ),
    )(start, tokens_in, gain, weight_t, ids_t, teacher_t, labels)


def local(tokens_in, gain, head_weight, teacher_ids, teacher_weight, labels):
    tokens, features = tokens_in.shape
    col_width = head_weight.shape[1]
    n_vocab = NY * NX
    block = lax.axis_index("y") * NX + lax.axis_index("x")
    core = lax.axis_index("c")
    swap = [(0, 1), (1, 0)]
    weight_t = head_weight.T
    start = (block * col_width).astype(jnp.int32).reshape(1)
    low, high, row_scale, logits, target, stats = front(
        tokens_in, gain[None], weight_t, teacher_ids.T, teacher_weight.T, labels[None], start, n_vocab
    )
    both_low = jnp.concatenate([low, lax.ppermute(low, "c", swap)], axis=0)
    both_high = jnp.concatenate([high, lax.ppermute(high, "c", swap)], axis=0)
    teacher_probs = teacher_weight / jnp.sum(teacher_weight, axis=1, keepdims=True)
    stats = lax.all_to_all(stats, ("y", "x"), 0, 0)
    row_top = jnp.max(stats[:, 0], axis=0)
    weight = jnp.exp(stats[:, 0] - row_top[None])
    total_exp = jnp.sum(weight * stats[:, 1], axis=0)
    total_dot = jnp.sum(stats[:, 2], axis=0)
    mean_logit = jnp.sum(weight * stats[:, 3], axis=0) / total_exp
    lse = row_top + jnp.log(total_exp)
    token_loss = (
        (1.0 - LABEL_SHARE) * jnp.sum(teacher_probs * jnp.log(teacher_probs), axis=1)
        - total_dot
        + lse
    )
    dlogits = (jnp.exp(logits - lse[None]) - target).astype(jnp.bfloat16)

    rows = col_width // (NZ * NC)
    by_owner = jnp.pad(dlogits.reshape(NZ, NC, rows, tokens), ((0, 0), (0, 0), (0, 2), (0, 0)))
    mine = lax.dynamic_index_in_dim(by_owner, core, 1, False).reshape(-1, tokens)
    theirs = lax.dynamic_index_in_dim(by_owner, 1 - core, 1, False).reshape(-1, tokens)
    other_mine = lax.ppermute(theirs, "c", swap)

    width = features // n_vocab
    partial_value = lax.dot_general(
        dlogits, weight_t, (((0,), (0,)), ((), ())), preferred_element_type=jnp.float32
    ).astype(jnp.bfloat16)
    pieces = partial_value.reshape(tokens, n_vocab, width).transpose(1, 0, 2)
    pieces = lax.all_to_all(pieces, ("y", "x"), 0, 0)

    factor = jnp.concatenate([mine, other_mine], axis=1)
    term1 = jnp.dot(factor, both_low, preferred_element_type=jnp.float32)
    summed1 = lax.psum_scatter(
        term1.astype(jnp.bfloat16), "z", scatter_dimension=0, tiled=True
    )[:rows]
    packed = factor.reshape(NZ, -1, 2 * tokens)[:, :rows].reshape(NZ * rows, 2 * tokens)
    term2 = jnp.dot(packed, both_high, preferred_element_type=jnp.float32)
    summed2 = lax.psum_scatter(
        term2.astype(jnp.bfloat16), "z", scatter_dimension=0, tiled=True
    )
    head_grad = jnp.concatenate([summed1, summed2], axis=1).astype(jnp.float32)[:, None, :]

    dhidden = jnp.sum(pieces.astype(jnp.float32), axis=0)
    local_tokens = lax.dynamic_slice_in_dim(tokens_in, block * width, width, 1).astype(jnp.float32)
    local_gain = lax.dynamic_slice_in_dim(gain, block * width, width, 0)
    inner_sum = row_scale * (mean_logit - total_dot)[:, None]
    cubed = row_scale * row_scale * row_scale
    grad_input = (
        dhidden * local_gain[None, :] / row_scale - local_tokens * inner_sum / (features * cubed)
    ).astype(jnp.bfloat16)
    return (token_loss, grad_input, head_grad)


def solution(mesh):
    fine = Mesh(mesh.devices.reshape(NZ, NC, NY, NX), ("z", "c", "y", "x"))
    dp, vocab = ("z", "c"), ("y", "x")
    in_specs = (P(dp, None), P(), P(None, vocab), P(dp, None), P(dp, None), P(dp))
    out_specs = (P(dp), P(dp, vocab), P(dp, vocab, None))
    return jax.shard_map(local, mesh=fine, in_specs=in_specs, out_specs=out_specs, check_vma=False)
```

```python
import jax
import jax.numpy as jnp
from jax import lax
from jax.experimental import pallas as pl
from jax.experimental.pallas import tpu as pltpu
from jax.sharding import Mesh, PartitionSpec as P


LABEL_SHARE = 0.5
EPS = 1e-05
NZ, NC, NY, NX = 12, 2, 8, 4


def front_kernel(
    start_ref, x_hbm, gain_ref, w_hbm, ids_ref, weight_ref, label_ref,
    normed_hbm, scale_ref, logits_ref, target_ref, stats_ref,
    x_buf, w_ref, normed_buf, x_sem, w_sem, out_sem,
):
    tokens, features = x_buf.shape
    cols = w_ref.shape[0]
    bounds = (0, 240, 432, cols)
    lines = 16
    copy_x = pltpu.make_async_copy(x_hbm, x_buf, x_sem)
    copy_x.start()

    def copy_w(p):
        part = pl.ds(bounds[p], bounds[p + 1] - bounds[p])
        return pltpu.make_async_copy(w_hbm.at[part], w_ref.at[part], w_sem.at[p])

    @pl.when(start_ref[0] >= 0)
    def _():
        for p in range(len(bounds) - 1):
            copy_w(p).start()

    probs = weight_ref[...] / jnp.sum(weight_ref[...], axis=0, keepdims=True)

    @pl.loop(0, cols // lines)
    def _(r):
        part = pl.ds(pl.multiple_of(r * lines, lines), lines)
        columns = start_ref[0] + r * lines + lax.broadcasted_iota(jnp.int32, (lines, tokens), 0)
        teacher_part = jnp.zeros((lines, tokens), jnp.float32)
        for k in range(ids_ref.shape[0]):
            teacher_part += jnp.where(ids_ref[k : k + 1, :] == columns, probs[k : k + 1, :], 0.0)
        label_part = jnp.where(label_ref[...] == columns, LABEL_SHARE, 0.0)
        target_ref[part, :] = (1.0 - LABEL_SHARE) * teacher_part + label_part

    copy_x.wait()

    @pl.loop(0, tokens // lines)
    def _(r):
        part = pl.ds(pl.multiple_of(r * lines, lines), lines)
        totals = [jnp.zeros((lines, 128), jnp.float32) for _ in range(4)]
        for f in range(0, features, 128):
            chunk = x_buf[part, f : f + 128].astype(jnp.float32)
            totals[f // 128 % 4] += chunk * chunk
        total = (totals[0] + totals[1]) + (totals[2] + totals[3])
        scale = jnp.sqrt(jnp.sum(total, axis=1, keepdims=True) / features + EPS)
        scale_ref[part, :] = scale
        inverse = jnp.broadcast_to(1.0 / scale, (lines, 128))
        for f in range(0, features, 128):
            chunk = x_buf[part, f : f + 128].astype(jnp.float32)
            chunk = chunk * inverse * gain_ref[:, f : f + 128]
            normed_buf[part, f : f + 128] = chunk.astype(jnp.bfloat16)

    copy_out = pltpu.make_async_copy(normed_buf, normed_hbm, out_sem)
    copy_out.start()
    for p in range(len(bounds) - 1):
        copy_w(p).wait()
        part = pl.ds(bounds[p], bounds[p + 1] - bounds[p])
        logits_ref[part, :] = lax.dot_general(
            w_ref[part, :],
            normed_buf[...],
            (((1,), (1,)), ((), ())),
            preferred_element_type=jnp.float32,
        )
    logits = logits_ref[...]
    top = jnp.max(logits, axis=0, keepdims=True)
    exps = jnp.exp(logits - top)
    local_stats = (
        top,
        jnp.sum(exps, axis=0, keepdims=True),
        jnp.sum(target_ref[...] * logits, axis=0, keepdims=True),
        jnp.sum(exps * logits, axis=0, keepdims=True),
    )
    for q, row in enumerate(local_stats):
        stats_ref[:, q, :] = jnp.broadcast_to(row, (stats_ref.shape[0], tokens))
    copy_out.wait()


def front(tokens_in, gain, weight_t, ids_t, teacher_t, labels, start, n_vocab):
    tokens, features = tokens_in.shape
    cols = weight_t.shape[0]
    vmem = pl.BlockSpec(memory_space=pltpu.VMEM)
    hbm = pl.BlockSpec(memory_space=pltpu.HBM)
    return pl.pallas_call(
        front_kernel,
        name="front",
        out_shape=(
            jax.ShapeDtypeStruct((tokens, features), jnp.bfloat16),
            jax.ShapeDtypeStruct((tokens, 1), jnp.float32),
            jax.ShapeDtypeStruct((cols, tokens), jnp.float32),
            jax.ShapeDtypeStruct((cols, tokens), jnp.float32),
            jax.ShapeDtypeStruct((n_vocab, 4, tokens), jnp.float32),
        ),
        in_specs=[pl.BlockSpec(memory_space=pltpu.SMEM), hbm, vmem, hbm, vmem, vmem, vmem],
        out_specs=(hbm, vmem, vmem, vmem, vmem),
        scratch_shapes=[
            pltpu.VMEM((tokens, features), jnp.bfloat16),
            pltpu.VMEM((cols, features), jnp.bfloat16),
            pltpu.VMEM((tokens, features), jnp.bfloat16),
            pltpu.SemaphoreType.DMA,
            pltpu.SemaphoreType.DMA((3,)),
            pltpu.SemaphoreType.DMA,
        ],
        cost_estimate=pl.CostEstimate(
            flops=2 * tokens * features * cols,
            bytes_accessed=2 * features * (2 * tokens + cols),
            transcendentals=cols * tokens,
        ),
    )(start, tokens_in, gain, weight_t, ids_t, teacher_t, labels)


def spread_kernel(in_ref, out_ref):
    for r in range(out_ref.shape[0]):
        if r % 8 == 0:
            lines = in_ref[r : r + 8, :].astype(jnp.float32)
        out_ref[r] = lines[r % 8 : r % 8 + 1, :]


def spread(summed, rows):
    features = summed.shape[1]
    step = 2048
    return pl.pallas_call(
        spread_kernel,
        name="spread",
        grid=(features // step,),
        out_shape=jax.ShapeDtypeStruct((rows, 1, features), jnp.float32),
        in_specs=[pl.BlockSpec((summed.shape[0], step), lambda i: (0, i))],
        out_specs=pl.BlockSpec((rows, 1, step), lambda i: (0, 0, i)),
        cost_estimate=pl.CostEstimate(
            flops=0, bytes_accessed=8 * rows * features, transcendentals=0
        ),
    )(summed)


def local(tokens_in, gain, head_weight, teacher_ids, teacher_weight, labels):
    tokens, features = tokens_in.shape
    col_width = head_weight.shape[1]
    n_vocab = NY * NX
    block = lax.axis_index("y") * NX + lax.axis_index("x")
    core = lax.axis_index("c")
    swap = [(0, 1), (1, 0)]
    weight_t = head_weight.T
    start = (block * col_width).astype(jnp.int32).reshape(1)
    normed, row_scale, logits, target, stats = front(
        tokens_in, gain[None], weight_t, teacher_ids.T, teacher_weight.T, labels[None], start, n_vocab
    )
    both = jnp.concatenate([normed, lax.ppermute(normed, "c", swap)], axis=0)
    teacher_probs = teacher_weight / jnp.sum(teacher_weight, axis=1, keepdims=True)
    stats = lax.all_to_all(stats, ("y", "x"), 0, 0)
    row_top = jnp.max(stats[:, 0], axis=0)
    weight = jnp.exp(stats[:, 0] - row_top[None])
    total_exp = jnp.sum(weight * stats[:, 1], axis=0)
    total_dot = jnp.sum(stats[:, 2], axis=0)
    mean_logit = jnp.sum(weight * stats[:, 3], axis=0) / total_exp
    lse = row_top + jnp.log(total_exp)
    token_loss = (
        (1.0 - LABEL_SHARE) * jnp.sum(teacher_probs * jnp.log(teacher_probs), axis=1)
        - total_dot
        + lse
    )
    dlogits = (jnp.exp(logits - lse[None]) - target).astype(jnp.bfloat16)

    rows = col_width // (NZ * NC)
    by_owner = jnp.pad(dlogits.reshape(NZ, NC, rows, tokens), ((0, 0), (0, 0), (0, 2), (0, 0)))
    mine = lax.dynamic_index_in_dim(by_owner, core, 1, False).reshape(-1, tokens)
    theirs = lax.dynamic_index_in_dim(by_owner, 1 - core, 1, False).reshape(-1, tokens)
    other_mine = lax.ppermute(theirs, "c", swap)

    width = features // n_vocab
    partial_value = lax.dot_general(
        dlogits, weight_t, (((0,), (0,)), ((), ())), preferred_element_type=jnp.float32
    ).astype(jnp.bfloat16)
    pieces = partial_value.reshape(tokens, n_vocab, width).transpose(1, 0, 2)
    pieces = lax.all_to_all(pieces, ("y", "x"), 0, 0)

    factor = jnp.concatenate([mine, other_mine], axis=1)
    head_term = jnp.dot(factor, both, preferred_element_type=jnp.float32)
    summed = lax.psum_scatter(head_term.astype(jnp.bfloat16), "z", scatter_dimension=0, tiled=True)
    head_grad = spread(summed, rows)

    dhidden = jnp.sum(pieces.astype(jnp.float32), axis=0)
    local_tokens = lax.dynamic_slice_in_dim(tokens_in, block * width, width, 1).astype(jnp.float32)
    local_gain = lax.dynamic_slice_in_dim(gain, block * width, width, 0)
    inner_sum = row_scale * (mean_logit - total_dot)[:, None]
    cubed = row_scale * row_scale * row_scale
    grad_input = (
        dhidden * local_gain[None, :] / row_scale - local_tokens * inner_sum / (features * cubed)
    ).astype(jnp.bfloat16)
    return (token_loss, grad_input, head_grad)


def solution(mesh):
    fine = Mesh(mesh.devices.reshape(NZ, NC, NY, NX), ("z", "c", "y", "x"))
    dp, vocab = ("z", "c"), ("y", "x")
    in_specs = (P(dp, None), P(), P(None, vocab), P(dp, None), P(dp, None), P(dp))
    out_specs = (P(dp), P(dp, vocab), P(dp, vocab, None))
    return jax.shard_map(local, mesh=fine, in_specs=in_specs, out_specs=out_specs, check_vma=False)
```

```python
import jax
import jax.numpy as jnp
from jax import lax
from jax.experimental import pallas as pl
from jax.experimental.pallas import tpu as pltpu
from jax.sharding import Mesh, PartitionSpec as P


LABEL_SHARE = 0.5
EPS = 1e-05
NZ, NC, NY, NX = 12, 2, 8, 4


def front_kernel(
    start_ref, x_hbm, gain_ref, w_hbm, ids_ref, weight_ref, label_ref,
    normed_hbm, scale_ref, logits_ref, target_ref, stats_ref,
    x_buf, w_ref, normed_buf, x_sem, w_sem, out_sem,
):
    tokens, features = x_buf.shape
    cols = w_ref.shape[0]
    parts = w_sem.shape[0]
    rows = cols // parts
    lines = 16
    copy_x = pltpu.make_async_copy(x_hbm, x_buf, x_sem)
    copy_x.start()

    def copy_w(p):
        part = pl.ds(p * rows, rows)
        return pltpu.make_async_copy(w_hbm.at[part], w_ref.at[part], w_sem.at[p])

    @pl.loop(0, parts)
    def _(p):
        copy_w(p).start()

    probs = weight_ref[...] / jnp.sum(weight_ref[...], axis=0, keepdims=True)

    @pl.loop(0, cols // lines)
    def _(r):
        part = pl.ds(pl.multiple_of(r * lines, lines), lines)
        columns = start_ref[0] + r * lines + lax.broadcasted_iota(jnp.int32, (lines, tokens), 0)
        teacher_part = jnp.zeros((lines, tokens), jnp.float32)
        for k in range(ids_ref.shape[0]):
            teacher_part += jnp.where(ids_ref[k : k + 1, :] == columns, probs[k : k + 1, :], 0.0)
        label_part = jnp.where(label_ref[...] == columns, LABEL_SHARE, 0.0)
        target_ref[part, :] = (1.0 - LABEL_SHARE) * teacher_part + label_part

    copy_x.wait()

    @pl.loop(0, tokens // lines)
    def _(r):
        part = pl.ds(pl.multiple_of(r * lines, lines), lines)
        totals = [jnp.zeros((lines, 128), jnp.float32) for _ in range(4)]
        for f in range(0, features, 128):
            chunk = x_buf[part, f : f + 128].astype(jnp.float32)
            totals[f // 128 % 4] += chunk * chunk
        total = (totals[0] + totals[1]) + (totals[2] + totals[3])
        scale = jnp.sqrt(jnp.sum(total, axis=1, keepdims=True) / features + EPS)
        scale_ref[part, :] = scale
        inverse = jnp.broadcast_to(1.0 / scale, (lines, 128))
        for f in range(0, features, 128):
            chunk = x_buf[part, f : f + 128].astype(jnp.float32)
            chunk = chunk * inverse * gain_ref[:, f : f + 128]
            normed_buf[part, f : f + 128] = chunk.astype(jnp.bfloat16)

    copy_out = pltpu.make_async_copy(normed_buf, normed_hbm, out_sem)
    copy_out.start()
    for p in range(parts):
        copy_w(p).wait()
        part = pl.ds(p * rows, rows)
        logits_ref[part, :] = lax.dot_general(
            w_ref[part, :],
            normed_buf[...],
            (((1,), (1,)), ((), ())),
            preferred_element_type=jnp.float32,
        )
    logits = logits_ref[...]
    top = jnp.max(logits, axis=0, keepdims=True)
    exps = jnp.exp(logits - top)
    local_stats = (
        top,
        jnp.sum(exps, axis=0, keepdims=True),
        jnp.sum(target_ref[...] * logits, axis=0, keepdims=True),
        jnp.sum(exps * logits, axis=0, keepdims=True),
    )
    for q, row in enumerate(local_stats):
        stats_ref[:, q, :] = jnp.broadcast_to(row, (stats_ref.shape[0], tokens))
    copy_out.wait()


def front(tokens_in, gain, weight_t, ids_t, teacher_t, labels, start, n_vocab):
    tokens, features = tokens_in.shape
    cols = weight_t.shape[0]
    vmem = pl.BlockSpec(memory_space=pltpu.VMEM)
    hbm = pl.BlockSpec(memory_space=pltpu.HBM)
    return pl.pallas_call(
        front_kernel,
        name="front",
        out_shape=(
            jax.ShapeDtypeStruct((tokens, features), jnp.bfloat16),
            jax.ShapeDtypeStruct((tokens, 1), jnp.float32),
            jax.ShapeDtypeStruct((cols, tokens), jnp.float32),
            jax.ShapeDtypeStruct((cols, tokens), jnp.float32),
            jax.ShapeDtypeStruct((n_vocab, 4, tokens), jnp.float32),
        ),
        in_specs=[pl.BlockSpec(memory_space=pltpu.SMEM), hbm, vmem, hbm, vmem, vmem, vmem],
        out_specs=(hbm, vmem, vmem, vmem, vmem),
        scratch_shapes=[
            pltpu.VMEM((tokens, features), jnp.bfloat16),
            pltpu.VMEM((cols, features), jnp.bfloat16),
            pltpu.VMEM((tokens, features), jnp.bfloat16),
            pltpu.SemaphoreType.DMA,
            pltpu.SemaphoreType.DMA((3,)),
            pltpu.SemaphoreType.DMA,
        ],
        cost_estimate=pl.CostEstimate(
            flops=2 * tokens * features * cols,
            bytes_accessed=2 * features * (2 * tokens + cols),
            transcendentals=cols * tokens,
        ),
    )(start, tokens_in, gain, weight_t, ids_t, teacher_t, labels)


def local(tokens_in, gain, head_weight, teacher_ids, teacher_weight, labels):
    tokens, features = tokens_in.shape
    col_width = head_weight.shape[1]
    n_vocab = NY * NX
    block = lax.axis_index("y") * NX + lax.axis_index("x")
    core = lax.axis_index("c")
    swap = [(0, 1), (1, 0)]
    weight_t = head_weight.T
    start = (block * col_width).astype(jnp.int32).reshape(1)
    normed, row_scale, logits, target, stats = front(
        tokens_in, gain[None], weight_t, teacher_ids.T, teacher_weight.T, labels[None], start, n_vocab
    )
    both = jnp.concatenate([normed, lax.ppermute(normed, "c", swap)], axis=0)
    teacher_probs = teacher_weight / jnp.sum(teacher_weight, axis=1, keepdims=True)
    stats = lax.all_to_all(stats, ("y", "x"), 0, 0)
    row_top = jnp.max(stats[:, 0], axis=0)
    weight = jnp.exp(stats[:, 0] - row_top[None])
    total_exp = jnp.sum(weight * stats[:, 1], axis=0)
    total_dot = jnp.sum(stats[:, 2], axis=0)
    mean_logit = jnp.sum(weight * stats[:, 3], axis=0) / total_exp
    lse = row_top + jnp.log(total_exp)
    token_loss = (
        (1.0 - LABEL_SHARE) * jnp.sum(teacher_probs * jnp.log(teacher_probs), axis=1)
        - total_dot
        + lse
    )
    dlogits = (jnp.exp(logits - lse[None]) - target).astype(jnp.bfloat16)

    rows = col_width // (NZ * NC)
    by_owner = jnp.pad(dlogits.reshape(NZ, NC, rows, tokens), ((0, 0), (0, 0), (0, 1), (0, 0)))
    mine = lax.dynamic_index_in_dim(by_owner, core, 1, False).reshape(-1, tokens)
    theirs = lax.dynamic_index_in_dim(by_owner, 1 - core, 1, False).reshape(-1, tokens)
    other_mine = lax.ppermute(theirs, "c", swap)

    width = features // n_vocab
    partial_value = lax.dot_general(
        dlogits, weight_t, (((0,), (0,)), ((), ())), preferred_element_type=jnp.float32
    ).astype(jnp.bfloat16)
    pieces = partial_value.reshape(tokens, n_vocab, width).transpose(1, 0, 2)
    pieces = lax.all_to_all(pieces, ("y", "x"), 0, 0)

    factor = jnp.concatenate([mine, other_mine], axis=1)
    head_term = jnp.dot(factor, both, preferred_element_type=jnp.float32)
    summed = lax.psum_scatter(head_term.astype(jnp.bfloat16), "z", scatter_dimension=0, tiled=True)
    summed = lax.optimization_barrier(summed)
    head_grad = summed[:rows].astype(jnp.float32)[:, None, :]

    dhidden = jnp.sum(pieces.astype(jnp.float32), axis=0)
    local_tokens = lax.dynamic_slice_in_dim(tokens_in, block * width, width, 1).astype(jnp.float32)
    local_gain = lax.dynamic_slice_in_dim(gain, block * width, width, 0)
    inner_sum = row_scale * (mean_logit - total_dot)[:, None]
    cubed = row_scale * row_scale * row_scale
    grad_input = (
        dhidden * local_gain[None, :] / row_scale - local_tokens * inner_sum / (features * cubed)
    ).astype(jnp.bfloat16)
    return (token_loss, grad_input, head_grad)


def solution(mesh):
    fine = Mesh(mesh.devices.reshape(NZ, NC, NY, NX), ("z", "c", "y", "x"))
    dp, vocab = ("z", "c"), ("y", "x")
    in_specs = (P(dp, None), P(), P(None, vocab), P(dp, None), P(dp, None), P(dp))
    out_specs = (P(dp), P(dp, vocab), P(dp, vocab, None))
    return jax.shard_map(local, mesh=fine, in_specs=in_specs, out_specs=out_specs, check_vma=False)
```

```python
import jax
import jax.numpy as jnp
from jax import lax
from jax.experimental import pallas as pl
from jax.experimental.pallas import tpu as pltpu
from jax.sharding import Mesh, PartitionSpec as P


LABEL_SHARE = 0.5
EPS = 1e-05
NZ, NC, NY, NX = 12, 2, 8, 4


def front_kernel(
    start_ref, x_hbm, gain_ref, w_hbm, ids_ref, weight_ref, label_ref,
    normed_hbm, scale_ref, logits_ref, target_ref, stats_ref,
    x_buf, w_ref, normed_buf, x_sem, w_sem, out_sem,
):
    tokens, features = x_buf.shape
    cols = w_ref.shape[0]
    parts = w_sem.shape[0]
    rows = cols // parts
    lines = 16
    copy_x = pltpu.make_async_copy(x_hbm, x_buf, x_sem)
    copy_x.start()

    def copy_w(p):
        part = pl.ds(p * rows, rows)
        return pltpu.make_async_copy(w_hbm.at[part], w_ref.at[part], w_sem.at[p])

    @pl.loop(0, parts)
    def _(p):
        copy_w(p).start()

    probs = weight_ref[...] / jnp.sum(weight_ref[...], axis=0, keepdims=True)

    @pl.loop(0, cols // lines)
    def _(r):
        part = pl.ds(pl.multiple_of(r * lines, lines), lines)
        columns = start_ref[0] + r * lines + lax.broadcasted_iota(jnp.int32, (lines, tokens), 0)
        teacher_part = jnp.zeros((lines, tokens), jnp.float32)
        for k in range(ids_ref.shape[0]):
            teacher_part += jnp.where(ids_ref[k : k + 1, :] == columns, probs[k : k + 1, :], 0.0)
        label_part = jnp.where(label_ref[...] == columns, LABEL_SHARE, 0.0)
        target_ref[part, :] = (1.0 - LABEL_SHARE) * teacher_part + label_part

    copy_x.wait()

    @pl.loop(0, tokens // lines)
    def _(r):
        part = pl.ds(pl.multiple_of(r * lines, lines), lines)
        totals = [jnp.zeros((lines, 128), jnp.float32) for _ in range(4)]
        for f in range(0, features, 128):
            chunk = x_buf[part, f : f + 128].astype(jnp.float32)
            totals[f // 128 % 4] += chunk * chunk
        total = (totals[0] + totals[1]) + (totals[2] + totals[3])
        scale = jnp.sqrt(jnp.sum(total, axis=1, keepdims=True) / features + EPS)
        scale_ref[part, :] = scale
        inverse = jnp.broadcast_to(1.0 / scale, (lines, 128))
        for f in range(0, features, 128):
            chunk = x_buf[part, f : f + 128].astype(jnp.float32)
            chunk = chunk * inverse * gain_ref[:, f : f + 128]
            normed_buf[part, f : f + 128] = chunk.astype(jnp.bfloat16)

    copy_out = pltpu.make_async_copy(normed_buf, normed_hbm, out_sem)
    copy_out.start()
    for p in range(parts):
        copy_w(p).wait()
        part = pl.ds(p * rows, rows)
        logits_ref[part, :] = lax.dot_general(
            w_ref[part, :],
            normed_buf[...],
            (((1,), (1,)), ((), ())),
            preferred_element_type=jnp.float32,
        )
    logits = logits_ref[...]
    top = jnp.max(logits, axis=0, keepdims=True)
    exps = jnp.exp(logits - top)
    local_stats = (
        top,
        jnp.sum(exps, axis=0, keepdims=True),
        jnp.sum(target_ref[...] * logits, axis=0, keepdims=True),
        jnp.sum(exps * logits, axis=0, keepdims=True),
    )
    for q, row in enumerate(local_stats):
        stats_ref[:, q, :] = jnp.broadcast_to(row, (stats_ref.shape[0], tokens))
    copy_out.wait()


def front(tokens_in, gain, weight_t, ids_t, teacher_t, labels, start, n_vocab):
    tokens, features = tokens_in.shape
    cols = weight_t.shape[0]
    vmem = pl.BlockSpec(memory_space=pltpu.VMEM)
    hbm = pl.BlockSpec(memory_space=pltpu.HBM)
    return pl.pallas_call(
        front_kernel,
        name="front",
        out_shape=(
            jax.ShapeDtypeStruct((tokens, features), jnp.bfloat16),
            jax.ShapeDtypeStruct((tokens, 1), jnp.float32),
            jax.ShapeDtypeStruct((cols, tokens), jnp.float32),
            jax.ShapeDtypeStruct((cols, tokens), jnp.float32),
            jax.ShapeDtypeStruct((n_vocab, 4, tokens), jnp.float32),
        ),
        in_specs=[pl.BlockSpec(memory_space=pltpu.SMEM), hbm, vmem, hbm, vmem, vmem, vmem],
        out_specs=(hbm, vmem, vmem, vmem, vmem),
        scratch_shapes=[
            pltpu.VMEM((tokens, features), jnp.bfloat16),
            pltpu.VMEM((cols, features), jnp.bfloat16),
            pltpu.VMEM((tokens, features), jnp.bfloat16),
            pltpu.SemaphoreType.DMA,
            pltpu.SemaphoreType.DMA((3,)),
            pltpu.SemaphoreType.DMA,
        ],
        cost_estimate=pl.CostEstimate(
            flops=2 * tokens * features * cols,
            bytes_accessed=2 * features * (2 * tokens + cols),
            transcendentals=cols * tokens,
        ),
    )(start, tokens_in, gain, weight_t, ids_t, teacher_t, labels)


def local(tokens_in, gain, head_weight, teacher_ids, teacher_weight, labels):
    tokens, features = tokens_in.shape
    col_width = head_weight.shape[1]
    n_vocab = NY * NX
    block = lax.axis_index("y") * NX + lax.axis_index("x")
    core = lax.axis_index("c")
    swap = [(0, 1), (1, 0)]
    weight_t = head_weight.T
    start = (block * col_width).astype(jnp.int32).reshape(1)
    normed, row_scale, logits, target, stats = front(
        tokens_in, gain[None], weight_t, teacher_ids.T, teacher_weight.T, labels[None], start, n_vocab
    )
    both = jnp.concatenate([normed, lax.ppermute(normed, "c", swap)], axis=0)
    teacher_probs = teacher_weight / jnp.sum(teacher_weight, axis=1, keepdims=True)
    stats = lax.all_to_all(stats, ("y", "x"), 0, 0)
    row_top = jnp.max(stats[:, 0], axis=0)
    weight = jnp.exp(stats[:, 0] - row_top[None])
    total_exp = jnp.sum(weight * stats[:, 1], axis=0)
    total_dot = jnp.sum(stats[:, 2], axis=0)
    mean_logit = jnp.sum(weight * stats[:, 3], axis=0) / total_exp
    lse = row_top + jnp.log(total_exp)
    token_loss = (
        (1.0 - LABEL_SHARE) * jnp.sum(teacher_probs * jnp.log(teacher_probs), axis=1)
        - total_dot
        + lse
    )
    dlogits = (jnp.exp(logits - lse[None]) - target).astype(jnp.bfloat16)

    rows = col_width // (NZ * NC)
    by_owner = jnp.pad(dlogits.reshape(NZ, NC, rows, tokens), ((0, 0), (0, 0), (0, 2), (0, 0)))
    mine = lax.dynamic_index_in_dim(by_owner, core, 1, False).reshape(-1, tokens)
    theirs = lax.dynamic_index_in_dim(by_owner, 1 - core, 1, False).reshape(-1, tokens)
    other_mine = lax.ppermute(theirs, "c", swap)

    width = features // n_vocab
    partial_value = lax.dot_general(
        dlogits, weight_t, (((0,), (0,)), ((), ())), preferred_element_type=jnp.float32
    ).astype(jnp.bfloat16)
    pieces = partial_value.reshape(tokens, n_vocab, width).transpose(1, 0, 2)
    pieces = lax.all_to_all(pieces, ("y", "x"), 0, 0)

    factor = jnp.concatenate([mine.T, other_mine.T], axis=0)
    head_term = lax.dot_general(
        factor, both, (((0,), (0,)), ((), ())), preferred_element_type=jnp.float32
    )
    summed = lax.psum_scatter(head_term.astype(jnp.bfloat16), "z", scatter_dimension=0, tiled=True)
    head_grad = summed[:rows].astype(jnp.float32)[:, None, :]

    dhidden = jnp.sum(pieces.astype(jnp.float32), axis=0)
    local_tokens = lax.dynamic_slice_in_dim(tokens_in, block * width, width, 1).astype(jnp.float32)
    local_gain = lax.dynamic_slice_in_dim(gain, block * width, width, 0)
    inner_sum = row_scale * (mean_logit - total_dot)[:, None]
    cubed = row_scale * row_scale * row_scale
    grad_input = (
        dhidden * local_gain[None, :] / row_scale - local_tokens * inner_sum / (features * cubed)
    ).astype(jnp.bfloat16)
    return (token_loss, grad_input, head_grad)


def solution(mesh):
    fine = Mesh(mesh.devices.reshape(NZ, NC, NY, NX), ("z", "c", "y", "x"))
    dp, vocab = ("z", "c"), ("y", "x")
    in_specs = (P(dp, None), P(), P(None, vocab), P(dp, None), P(dp, None), P(dp))
    out_specs = (P(dp), P(dp, vocab), P(dp, vocab, None))
    return jax.shard_map(local, mesh=fine, in_specs=in_specs, out_specs=out_specs, check_vma=False)
```
